32 devices in a mesh: tm: 16 (over z, y, x), sensor: 2 (over core).
Axes of the slice: x: 2, y: 2, z: 4, core: 2. Of those that a mesh axis runs over, the one named last changes fastest.
Arguments:
- sensor_rows: float32 [4096, 128], P('sensor'), may hold values from -0.12 to 0.12
- sensor_prec: float32 [4096], P('sensor'), may hold values from 0.5 to 2
- obs_sensor: int32 [8192], P(('tm', 'sensor')), may hold values from 0 to 2047
- obs_value: float32 [8192], P(('tm', 'sensor')), may hold values from -6 to 6
- obs_block: int32 [8192, 1], P(('tm', 'sensor')), may hold values from 0 to 15; in each aligned block of 256 rows (0 to 255, 256 to 511, ...) at most 32 rows name the same one
- obs_offset: int32 [8192], P(('tm', 'sensor')), may hold values from 0 to 63
- decay: float32 [1024, 128], P('tm'), may hold values from 0 to 1, as said below
- mix_raw: float32 [128, 128], replicated, may hold values from -1.2 to 1.2
- combine: float32 [128, 128], replicated, may hold values from -0.5 to 0.5
Outputs:
- smoothed: float32 [1024, 128], P('tm')
The draws below stay inside these ranges and needn't reach their ends.
Inputs may be any that keep to these rules, and one draw needn't show every extreme that they name: `decay`: every factor lies in (0, 1]. `obs_block`: the rows of one device name one time block at most 32 times, and exactly 32 times for some block.
All inputs are finite; a program needn't handle non-finite values.
Results may differ from the reference program's by a relative error of at most 0.007.
Values may be sent and summed in bfloat16 or wider, within the bound.
A program may use at most 128 MiB of HBM per device.

```python
import math
import jax
import jax.numpy as jnp
import numpy as np
from jax import lax

STATE_WIDTH = 128
STEPS_DEV = 64
SENSORS = 4096
ROTATION_ITERS = 12
TOTAL_TIME_STEPS = 1024
OBS_DEV = 256
OBS = 8192
CAP = 32
SENS_GRP = 2048
N_TM = 16
N_SENSOR = 2


def component_classes(key):
    slow_share = 50
    class_draws = jax.random.randint(jax.random.fold_in(key, 101), (STATE_WIDTH,), 0, 100)
    return (class_draws < slow_share).astype(jnp.int32)


def draw_decay(key, part):
    random_seed_keys = jax.random.split(jax.random.fold_in(key, 202), 5)
    slow_flags = component_classes(key)
    step_total = 1.0 * TOTAL_TIME_STEPS
    slowrate = jnp.exp(jax.random.uniform(random_seed_keys[0], (STATE_WIDTH,), jnp.float32, jnp.log(0.002 / step_total), jnp.log(0.2 / step_total)))
    fastrate = jnp.exp(jax.random.uniform(random_seed_keys[1], (STATE_WIDTH,), jnp.float32, jnp.log(1.0 / 50.0), jnp.log(1.0 / 30.0)))
    damping_factors = jnp.where(slow_flags == 1, slowrate, fastrate)
    jaggedness = jax.random.uniform(random_seed_keys[2], (TOTAL_TIME_STEPS, STATE_WIDTH), jnp.float32, 0.5, 1.5)
    surge_mask = jax.random.uniform(random_seed_keys[3], (TOTAL_TIME_STEPS, STATE_WIDTH)) < 2.0 / step_total
    surge_length = jax.random.uniform(random_seed_keys[4], (TOTAL_TIME_STEPS, STATE_WIDTH), jnp.float32, 0.5, 0.8)
    surge_multiplier = jnp.where(surge_mask, surge_length, 1.0)
    return (jnp.exp(-damping_factors[None, :] * jaggedness) * surge_multiplier).astype(jnp.float32)


def draw_mix_raw(key, part):
    random_seed_keys = jax.random.split(jax.random.fold_in(key, 303), 4)
    slow_flags = component_classes(key)
    scores = jax.random.permutation(random_seed_keys[0], STATE_WIDTH).astype(jnp.int32)
    sort_keys = slow_flags * STATE_WIDTH + scores
    ordering = jnp.argsort(sort_keys, stable=True).astype(jnp.int32)
    fast_count = STATE_WIDTH - jnp.sum(slow_flags)
    position = jnp.arange(STATE_WIDTH, dtype=jnp.int32)
    sorted_class = slow_flags[ordering]
    segment_start = jnp.where(sorted_class == 1, fast_count, 0)
    segment_size = jnp.where(sorted_class == 1, STATE_WIDTH - fast_count, fast_count)
    successor_pos = segment_start + (position - segment_start + 1) % segment_size
    successor_sorted = ordering[successor_pos]
    inverse = jnp.argsort(ordering, stable=True).astype(jnp.int32)
    successor = successor_sorted[inverse]
    sign_values = (2 * jax.random.randint(random_seed_keys[1], (STATE_WIDTH,), 0, 2) - 1).astype(jnp.float32)
    signed_shift = (position[:, None] == successor[None, :]).astype(jnp.float32) * sign_values[None, :]
    same_class = (slow_flags[:, None] == slow_flags[None, :]).astype(jnp.float32)
    jitter = jnp.clip(jax.random.normal(random_seed_keys[2], (STATE_WIDTH, STATE_WIDTH), jnp.float32), -4.0, 4.0)
    row_scale = jnp.exp(jax.random.uniform(random_seed_keys[3], (STATE_WIDTH, 1), jnp.float32, jnp.log(0.15), 0.0))
    return (row_scale * (signed_shift + 0.25 * jitter * same_class / jnp.sqrt(1.0 * STATE_WIDTH))).astype(jnp.float32)


def touch_ends(values, rng, low, high):
    longest = values.shape.index(max(values.shape))
    spots = []
    for shift in (0, 1):
        where = [jax.random.randint(jax.random.fold_in(rng, axis), (), 0, length) for axis, length in enumerate(values.shape)]
        where[longest] = (where[longest] + shift) % values.shape[longest]
        spots.append(tuple(where))
    return values.at[spots[0]].set(low).at[spots[1]].set(high)


def block_scale(rng, extent, shards, smallest, largest):
    loudness, own = 1.0, jax.random.fold_in(rng, 6)
    for dim, blocks in shards:
        heights = jnp.exp(jax.random.uniform(jax.random.fold_in(own, dim), (blocks,), jnp.float32, smallest / len(shards), largest / len(shards)))
        loudness = loudness * jnp.repeat(heights, extent[dim] // blocks).reshape([-1 if axis == dim else 1 for axis in range(len(extent))])
    return loudness


def routed_block(key, own, number, rows, number_of, top, reach, skew):
    sequence = jax.random.permutation(key, number_of)
    crowded, ordinary = portions_of(number_of, rows * top, reach, skew, True), portions_of(number_of, rows * top, reach, skew, False)
    places = jnp.arange(number_of)

    def named(lengths, turn):
        used = int((lengths > 0).sum())
        fixed = max(1, used // 4)
        moved = fixed + (places - fixed + turn * (used - fixed)) % max(1, number_of - fixed)
        return jnp.zeros((number_of,), jnp.int32).at[sequence[jnp.where(places < fixed, places, moved)]].set(jnp.asarray(lengths, jnp.int32))

    lengths = jnp.where(number % 4 == 0, named(crowded, number // 4), named(ordinary, number - number // 4 - 1))
    mixed = jax.random.permutation(jax.random.fold_in(own, 3), number_of)
    donor, sink = mixed[0:number_of // 2 * 2:2], mixed[1:number_of // 2 * 2:2]
    room = jnp.minimum(lengths[donor] - 1, reach - lengths[sink]) // 2
    room = jnp.where((donor == sequence[0]) | (sink == sequence[0]) | (lengths[sink] == 0), 0, jnp.maximum(room, 0))
    moved = jax.random.randint(jax.random.fold_in(own, 4), (number_of // 2,), 0, 1 << 20) % (room + 1)
    lengths = lengths.at[donor].add(-moved).at[sink].add(moved)
    labels = jnp.searchsorted(jnp.cumsum(lengths), jnp.arange(rows * top), side="right").astype(jnp.int32)
    table = labels.reshape(top, rows).T
    table = table[jax.random.permutation(jax.random.fold_in(own, 1), rows)]
    turn = jax.random.randint(jax.random.fold_in(own, 2), (rows, 1), 0, top)
    return jnp.take_along_axis(table, (jnp.arange(top)[None, :] + turn) % top, axis=1)


def portions_of(amount, total, limit, lean, full):
    portions = [(1 << 20) // math.isqrt(grade ** lean) + 1 for grade in range(1, amount + 1)]
    largest = limit if full else min(limit, max(-(-total // amount), total * portions[0] // sum(portions)))
    least = 1 if total - largest >= amount - 1 else 0
    counts, surplus = [largest] + [least] * (amount - 1), total - largest - least * (amount - 1)
    while surplus > 0:
        free = [i for i in range(1, amount) if counts[i] < largest] or [i for i in range(1, amount) if counts[i] < limit]
        mass, left = sum([portions[i] for i in free]), surplus
        for i in free:
            more = min(limit - counts[i], max(1, left * portions[i] // mass), surplus)
            counts[i] = counts[i] + more
            surplus = surplus - more
    return np.array(counts)


def scatter_about(own_key, extent, scale, reach, cuts=(), kind=jnp.bfloat16):
    drawn = jax.random.normal(own_key, extent, jnp.float32) * scale
    if len(cuts) > 0:
        drawn = block_scale(own_key, extent, cuts, -0.22, 0.18) * drawn
    return jnp.clip(drawn, min=-reach, max=reach).astype(kind)


def setup_inputs(seed: int = 0) -> dict:
    seeds = jax.random.split(jax.random.key(seed), 10)
    sensor_rows = scatter_about(seeds[0], (SENSORS, STATE_WIDTH), 0.02, 0.12, ((0, 2),), jnp.float32)
    sensor_prec = jnp.clip(jnp.exp(math.log(2.0) - 1.3862944 * jax.random.uniform(seeds[1], (SENSORS,), jnp.float32) ** block_scale(seeds[1], (SENSORS,), ((0, 2),), -0.2, 0.2)), 0.5, 2.0)
    obs_sensor = touch_ends(jax.random.randint(seeds[2], (OBS,), 0, SENS_GRP), jax.random.fold_in(seeds[2], 1), 0, SENS_GRP - 1).astype(jnp.int32)
    obs_value = scatter_about(seeds[3], (OBS,), 1.0, 6.0, ((0, 32),), jnp.float32)
    obs_block_keys = jax.random.split(jax.random.fold_in(seeds[4], 1), OBS // OBS_DEV)
    obs_block_turns = jax.random.permutation(jax.random.fold_in(seeds[4], 3), OBS // OBS_DEV)
    obs_block = jax.vmap(lambda own, number: routed_block(jax.random.fold_in(seeds[4], 2), own, number, OBS_DEV, N_TM, 1, CAP, 2))(obs_block_keys, obs_block_turns).reshape((OBS, 1))
    obs_offset = touch_ends(jax.random.randint(seeds[5], (OBS,), 0, STEPS_DEV), jax.random.fold_in(seeds[5], 1), 0, STEPS_DEV - 1).astype(jnp.int32)
    decay = draw_decay(jax.random.fold_in(seeds[9], 71), 0)
    mix_raw = draw_mix_raw(jax.random.fold_in(seeds[9], 71), 0)
    combine = scatter_about(seeds[8], (STATE_WIDTH, STATE_WIDTH), STATE_WIDTH ** -0.5, 0.5, (), jnp.float32)
    return dict(sensor_rows=sensor_rows, sensor_prec=sensor_prec, obs_sensor=obs_sensor, obs_value=obs_value, obs_block=obs_block, obs_offset=obs_offset, decay=decay, mix_raw=mix_raw, combine=combine)


HIGH = lax.Precision.HIGHEST


def polish(raw):
    matrix = raw
    for repeat in range(ROTATION_ITERS):
        square = jnp.matmul(matrix, matrix.T, precision=HIGH)
        matrix = 1.5 * matrix - 0.5 * jnp.matmul(square, matrix, precision=HIGH)
    return matrix


def reference(sensor_rows, sensor_prec, obs_sensor, obs_value, obs_block, obs_offset, decay, mix_raw, combine):
    rowids = jnp.arange(OBS, dtype=jnp.int32)
    groups = (rowids // OBS_DEV) % N_SENSOR
    sensors = groups * SENS_GRP + obs_sensor
    times = obs_block[:, 0] * STEPS_DEV + obs_offset
    contrib = (sensor_rows[sensors] * (obs_value * sensor_prec[sensors])[:, None]).astype(jnp.bfloat16)
    info = jax.ops.segment_sum(contrib.astype(jnp.float32), times, num_segments=TOTAL_TIME_STEPS)
    rotation = polish(mix_raw)

    def forward_step(carried, pieces):
        factor, incoming = pieces
        fresh = factor * jnp.matmul(rotation, carried, precision=HIGH) + incoming
        return fresh, fresh

    start = jnp.zeros((STATE_WIDTH,), jnp.float32)
    last, forward = lax.scan(forward_step, start, (decay, info))

    def backward_step(message, pieces):
        factor, incoming = pieces
        value = incoming + message
        return jnp.matmul(rotation.T, factor * value, precision=HIGH), value

    last, backward = lax.scan(backward_step, start, (decay, info), reverse=True)
    return jnp.matmul(forward + backward - info, combine, precision=HIGH)
```

```python
import functools
import math

import jax
import jax.numpy as jnp
from jax import lax
from jax.experimental import pallas as pl
from jax.experimental.pallas import tpu as pltpu
from jax.sharding import PartitionSpec as P

ROTATION_ITERS = 12
CHUNK = 8
F32, BF16 = jnp.float32, jnp.bfloat16
MESH = pl.DeviceIdType.MESH
NT = (((1,), (1,)), ((), ()))


def dot(x, y):
    return jnp.dot(x, y, preferred_element_type=F32)


def dot_nt(x, y):
    return lax.dot_general(x, y, NT, preferred_element_type=F32)


def cat(parts, axis):
    return jnp.concatenate(parts, axis=axis)


def split(x, n):
    parts = []
    for k in range(n):
        part = x.astype(BF16)
        parts.append(part)
        if k + 1 < n:
            x = x - part.astype(F32)
    return parts


def halves(z):
    w = z.shape[1] // 2
    return z[:, :w] + z[:, w:]


def lhs2(x):
    return cat(split(x, 2), 1)


def rhs2(y):
    row = cat(split(y, 2), 1)
    return cat([row, row], 0)


def rhs2_nt(y):
    a, b = split(y, 2)
    return cat([cat([a, a], 1), cat([b, b], 1)], 0)


def mm(x, y):
    return halves(dot(lhs2(x), rhs2(y)))


def mm_nt(x, y):
    return halves(dot_nt(lhs2(x), rhs2_nt(y)))


def polish(matrix):
    for _ in range(ROTATION_ITERS):
        a, b, c = split(matrix, 3)
        ab, ac = cat([a, b], 1), cat([a, c], 1)
        top = dot_nt(ab, cat([cat([a, a], 1), cat([b, b], 1)], 0))
        square = (dot_nt(ac, cat([c, a], 1)) + top[:, 128:]) + top[:, :128]
        p, q, r = split(square, 3)
        row = cat([a, b], 1)
        top = dot(cat([p, q], 1), cat([row, row], 0))
        cube = (dot(cat([p, r], 1), cat([c, a], 0)) + top[:, 128:]) + top[:, :128]
        matrix = 1.5 * matrix - 0.5 * cube
    return matrix


def kernel(
    inner, outer, cores,
    rows_ref, prec_ref, sens_ref, value_ref, block_ref, offset_ref, decay_ref, mix_ref, combine_ref,
    out_ref,
    part, got1, red1, got2, info, maps1, vecs1, maps2, vecs2, smooth,
    s_i1, r_i1, s_i2, r_i2, s_i3, r_i3, s_m1, r_m1, s_v1, r_v1, s_m2, r_m2, s_v2, r_v2,
):
    steps, width = decay_ref.shape
    half = steps // cores
    chunks = steps // CHUNK
    tm, core = lax.axis_index("tm"), lax.axis_index("sensor")
    mine, group = lax.rem(tm, inner), lax.div(tm, inner)
    spot = mine * cores + core
    spots = inner * cores

    def at_spot(s):
        return {"tm": group * inner + lax.div(s, cores), "sensor": lax.rem(s, cores)}

    def at_inner(k):
        return {"tm": group * inner + k, "sensor": core}

    def at_outer(k):
        return {"tm": k * inner + mine, "sensor": core}

    barrier = pltpu.get_barrier_semaphore()
    for r in range(1, spots):
        pl.semaphore_signal(barrier, inc=1, device_id=at_spot(lax.rem(spot + r, spots)), device_id_type=MESH)
    for r in range(1, outer):
        pl.semaphore_signal(barrier, inc=1, device_id=at_outer(lax.rem(group + r, outer)), device_id_type=MESH)

    obs = sens_ref.shape[1]
    column = jnp.broadcast_to(sens_ref[...].astype(F32), (width, obs)).T
    values = jnp.broadcast_to(value_ref[...], (width, obs)).T
    lane = lax.broadcasted_iota(jnp.int32, (obs, width), 1).astype(F32)
    hot, prec = [], jnp.zeros((obs, width), F32)
    for k in range(rows_ref.shape[0] // width):
        hit = (column - float(k * width)) == lane
        hot.append(jnp.where(hit, 1.0, 0.0).astype(BF16))
        prec = prec + jnp.where(hit, prec_ref[:, k * width : (k + 1) * width], 0.0)
    gain = values * jnp.sum(prec, axis=1, keepdims=True)
    picked = halves(dot(cat(hot, 1), lhs2(rows_ref[...])))
    contrib = (picked * gain).astype(BF16)

    block, offset = block_ref[...], offset_ref[...]
    place = ((lax.rem(block, inner) * cores + lax.div(offset, half)) * outer + lax.div(block, inner)) * half
    place = place + lax.rem(offset, half)
    size = outer * half
    for s in range(spots):
        line = lax.broadcasted_iota(jnp.int32, (size, obs), 0) + s * size
        part[s] = dot(jnp.where(line == place, 1.0, 0.0).astype(BF16), contrib).astype(BF16)

    pl.semaphore_wait(barrier, spots - 1 + outer - 1)

    sent1 = []
    for r in range(1, spots):
        to = lax.rem(spot + r, spots)
        copy = pltpu.make_async_remote_copy(
            part.at[to], got1.at[spot], s_i1.at[r], r_i1.at[r], device_id=at_spot(to), device_id_type=MESH
        )
        copy.start()
        sent1.append(copy)
    got1[spot] = part[spot]

    rotation = polish(mix_ref[...])
    turned = rotation.T
    ahead, back = rhs2(turned), rhs2(rotation)

    for copy in sent1:
        copy.wait()
    total = got1[0].astype(F32)
    for s in range(1, spots):
        total = total + got1[s].astype(F32)
    red1[...] = total.reshape(outer, half, width)
    sent2 = []
    for r in range(1, outer):
        to = lax.rem(group + r, outer)
        copy = pltpu.make_async_remote_copy(
            red1.at[to], got2.at[group], s_i2.at[r], r_i2.at[r], device_id=at_outer(to), device_id_type=MESH
        )
        copy.start()
        sent2.append(copy)
    got2[group] = red1[group]

    def decay_row(t):
        return decay_ref[t : t + 1, :]

    maps = [turned * decay_row(c * CHUNK) for c in range(chunks)]
    for j in range(1, CHUNK):
        maps = [halves(dot(lhs2(m), ahead)) * decay_row(c * CHUNK + j) for c, m in enumerate(maps)]

    for copy in sent2:
        copy.wait()
    total = got2[0]
    for k in range(1, outer):
        total = total + got2[k]
    info[core] = total
    other = cores - 1 - core
    copy3 = pltpu.make_async_remote_copy(
        info.at[core], info.at[core], s_i3, r_i3, device_id={"tm": tm, "sensor": other}, device_id_type=MESH
    )
    copy3.start()

    levels = [maps]
    while len(levels[-1]) > 1:
        last = levels[-1]
        levels.append([mm(last[k], last[k + 1]) for k in range(0, len(last), 2)])

    def exchange(source, slots, me, count, send, recv, place_of):
        copies = []
        for r in range(1, count):
            copy = pltpu.make_async_remote_copy(
                source, slots.at[me], send.at[r], recv.at[r],
                device_id=place_of(lax.rem(me + r, count)), device_id_type=MESH,
            )
            copy.start()
            copies.append(copy)
        return copies

    maps1[mine] = levels[-1][0]
    sent_m1 = exchange(maps1.at[mine], maps1, mine, inner, s_m1, r_m1, at_inner)

    copy3.wait()

    def strided(ref, j):
        return ref[pl.ds(j, chunks, stride=CHUNK), :]

    for c in range(cores):
        smooth[c * half : (c + 1) * half, :] = info[c]
    news = [strided(smooth, j) for j in range(CHUNK)]
    fades = [strided(decay_ref, j) for j in range(CHUNK)]

    def forward_scan(enter):
        out, state = [], enter
        for j in range(CHUNK):
            if state is None:
                state = news[j]
            else:
                state = halves(dot(lhs2(state), ahead)) * fades[j] + news[j]
            out.append(state)
        return out

    def backward_scan(arrive):
        out, message = [None] * CHUNK, arrive
        for j in reversed(range(CHUNK)):
            value = news[j] if message is None else news[j] + message
            out[j] = value
            message = halves(dot(lhs2(value * fades[j]), back))
        return out, message

    first = forward_scan(None)[-1]
    second = backward_scan(None)[1]
    fronts = [[first[c : c + 1] for c in range(chunks)]]
    tails = [[second[c : c + 1] for c in range(chunks)]]
    for depth in range(len(levels) - 1):
        f, b, m = fronts[-1], tails[-1], levels[depth]
        fronts.append([mm(f[k], m[k + 1]) + f[k + 1] for k in range(0, len(m), 2)])
        tails.append([mm_nt(b[k + 1], m[k]) + b[k] for k in range(0, len(m), 2)])

    vecs1[mine] = cat([fronts[-1][0], tails[-1][0], jnp.zeros((6, width), F32)], 0)
    sent_v1 = exchange(vecs1.at[mine], vecs1, mine, inner, s_v1, r_v1, at_inner)
    for copy in sent_m1:
        copy.wait()
    near = [maps1[k] for k in range(inner)]
    tree = [near]
    while len(tree[-1]) > 1:
        last = tree[-1]
        tree.append([mm(last[k], last[k + 1]) for k in range(0, len(last), 2)])
    maps2[group] = tree[-1][0]
    sent_m2 = exchange(maps2.at[group], maps2, group, outer, s_m2, r_m2, at_outer)
    for copy in sent_v1:
        copy.wait()
    f = [vecs1[k][0:1] for k in range(inner)]
    b = [vecs1[k][1:2] for k in range(inner)]
    near_f, near_b = f, b
    for depth in range(len(tree) - 1):
        m = tree[depth]
        f, b = (
            [mm(f[k], m[k + 1]) + f[k + 1] for k in range(0, len(m), 2)],
            [mm_nt(b[k + 1], m[k]) + b[k] for k in range(0, len(m), 2)],
        )
    vecs2[group] = cat([f[0], b[0], jnp.zeros((6, width), F32)], 0)
    sent_v2 = exchange(vecs2.at[group], vecs2, group, outer, s_v2, r_v2, at_outer)
    for copy in sent_m2 + sent_v2:
        copy.wait()

    enter = jnp.zeros((1, width), F32)
    arrive = jnp.zeros((1, width), F32)
    for k in range(outer - 1):
        enter = jnp.where(k < group, mm(enter, maps2[k]) + vecs2[k][0:1], enter)
        j = outer - 1 - k
        arrive = jnp.where(j > group, mm_nt(arrive, maps2[j]) + vecs2[j][1:2], arrive)
    for k in range(inner - 1):
        enter = jnp.where(k < mine, mm(enter, near[k]) + near_f[k], enter)
        j = inner - 1 - k
        arrive = jnp.where(j > mine, mm_nt(arrive, near[j]) + near_b[j], arrive)

    starts, ends = [enter], [arrive]
    for depth in reversed(range(len(levels) - 1)):
        m, f, b = levels[depth], fronts[depth], tails[depth]
        starts = [x for k, e in enumerate(starts) for x in (e, mm(e, m[2 * k]) + f[2 * k])]
        ends = [x for k, e in enumerate(ends) for x in (mm_nt(e, m[2 * k + 1]) + b[2 * k + 1], e)]
    start, end = cat(starts, 0), cat(ends, 0)
    forward = forward_scan(start)
    backward = backward_scan(end)[0]
    for j in range(CHUNK):
        smooth[pl.ds(j, chunks, stride=CHUNK), :] = forward[j] + backward[j] - news[j]
    out_ref[...] = mm(smooth[...], combine_ref[...])


def local(sensor_rows, sensor_prec, obs_sensor, obs_value, obs_block, obs_offset, decay, mix_raw, combine):
    peers, cores = lax.axis_size("tm"), lax.axis_size("sensor")
    inner = 1 << (int(math.log2(peers)) // 2)
    outer = peers // inner
    steps, width = decay.shape
    half = steps // cores
    spots = inner * cores
    dma = pltpu.SemaphoreType.DMA
    obs = obs_sensor.shape[0]
    return pl.pallas_call(
        functools.partial(kernel, inner, outer, cores),
        out_shape=jax.ShapeDtypeStruct((steps, width), F32),
        in_specs=[pl.BlockSpec(memory_space=pltpu.VMEM)] * 9,
        out_specs=pl.BlockSpec(memory_space=pltpu.VMEM),
        scratch_shapes=[
            pltpu.VMEM((spots, outer * half, width), BF16),
            pltpu.VMEM((spots, outer * half, width), BF16),
            pltpu.VMEM((outer, half, width), F32),
            pltpu.VMEM((outer, half, width), F32),
            pltpu.VMEM((cores, half, width), F32),
            pltpu.VMEM((inner, width, width), F32),
            pltpu.VMEM((inner, 8, width), F32),
            pltpu.VMEM((outer, width, width), F32),
            pltpu.VMEM((outer, 8, width), F32),
            pltpu.VMEM((steps, width), F32),
            dma((spots,)), dma((spots,)), dma((outer,)), dma((outer,)), dma, dma,
            dma((inner,)), dma((inner,)), dma((inner,)), dma((inner,)),
            dma((outer,)), dma((outer,)), dma((outer,)), dma((outer,)),
        ],
        compiler_params=pltpu.CompilerParams(
            collective_id=0, has_side_effects=True, vmem_limit_bytes=48 * 1024 * 1024
        ),
    )(
        sensor_rows, sensor_prec.reshape(1, -1), obs_sensor.reshape(1, obs), obs_value.reshape(1, obs),
        obs_block.reshape(1, obs), obs_offset.reshape(1, obs), decay, mix_raw, combine,
    )


def solution(mesh):
    placed = (
        P("sensor", None), P("sensor"), P(("tm", "sensor")), P(("tm", "sensor")),
        P(("tm", "sensor"), None), P(("tm", "sensor")), P("tm", None), P(), P(),
    )
    return jax.shard_map(local, mesh=mesh, in_specs=placed, out_specs=P("tm", None), check_vma=False)
```

```python
import functools
import math

import jax
import jax.numpy as jnp
from jax import lax
from jax.experimental import pallas as pl
from jax.experimental.pallas import tpu as pltpu
from jax.sharding import PartitionSpec as P

ROTATION_ITERS = 12
CHUNK = 8
F32, BF16 = jnp.float32, jnp.bfloat16
MESH = pl.DeviceIdType.MESH
NT = (((1,), (1,)), ((), ()))


def dot(x, y):
    return jnp.dot(x, y, preferred_element_type=F32)


def dot_nt(x, y):
    return lax.dot_general(x, y, NT, preferred_element_type=F32)


def cat(parts, axis):
    return jnp.concatenate(parts, axis=axis)


def split(x, n):
    parts = []
    for k in range(n):
        part = x.astype(BF16)
        parts.append(part)
        if k + 1 < n:
            x = x - part.astype(F32)
    return parts


def halves(z):
    w = z.shape[1] // 2
    return z[:, :w] + z[:, w:]


def lhs2(x):
    return cat(split(x, 2), 1)


def rhs2(y):
    row = cat(split(y, 2), 1)
    return cat([row, row], 0)


def rhs2_nt(y):
    a, b = split(y, 2)
    return cat([cat([a, a], 1), cat([b, b], 1)], 0)


def mm(x, y):
    return halves(dot(lhs2(x), rhs2(y)))


def mm_nt(x, y):
    return halves(dot_nt(lhs2(x), rhs2_nt(y)))


def polish_step(matrix):
    a, b, c = split(matrix, 3)
    ab, ac = cat([a, b], 1), cat([a, c], 1)
    top = dot_nt(ab, cat([cat([a, a], 1), cat([b, b], 1)], 0))
    square = (dot_nt(ac, cat([c, a], 1)) + top[:, 128:]) + top[:, :128]
    p, q, r = split(square, 3)
    top = dot(cat([p, q], 1), cat([ab, ab], 0))
    cube = (dot(cat([p, r], 1), cat([c, a], 0)) + top[:, 128:]) + top[:, :128]
    return 1.5 * matrix - 0.5 * cube


def kernel(
    inner, outer, cores, early,
    rows_hbm, prec_hbm, sens_hbm, value_hbm, block_hbm, offset_hbm, decay_hbm, mix_hbm, combine_hbm,
    out_ref,
    rows_ref, prec_ref, sens_ref, value_ref, block_ref, offset_ref, decay_ref, mix_ref, combine_ref, loads,
    part, got1, red1, got2, info, maps1, vecs1, maps2, vecs2, smooth, pairs, rows2,
    s_i1, r_i1, s_i2, r_i2, s_i3, r_i3, s_m1, r_m1, s_v1, r_v1, s_m2, r_m2, s_v2, r_v2,
):
    sources = (mix_hbm, sens_hbm, value_hbm, prec_hbm, block_hbm, offset_hbm, rows_hbm, decay_hbm, combine_hbm)
    targets = (mix_ref, sens_ref, value_ref, prec_ref, block_ref, offset_ref, rows_ref, decay_ref, combine_ref)
    copies_in = []
    for k, (source, target) in enumerate(zip(sources, targets)):
        copy = pltpu.make_async_copy(source, target, loads.at[k])
        copy.start()
        copies_in.append(copy)

    steps, width = decay_ref.shape
    half = steps // cores
    chunks = steps // CHUNK
    tm, core = lax.axis_index("tm"), lax.axis_index("sensor")
    mine, group = lax.rem(tm, inner), lax.div(tm, inner)
    spot = mine * cores + core
    spots = inner * cores

    def at_spot(s):
        return {"tm": group * inner + lax.div(s, cores), "sensor": lax.rem(s, cores)}

    def at_inner(k):
        return {"tm": group * inner + k, "sensor": core}

    def at_outer(k):
        return {"tm": k * inner + mine, "sensor": core}

    barrier = pltpu.get_barrier_semaphore()
    for r in range(1, spots):
        pl.semaphore_signal(barrier, inc=1, device_id=at_spot(lax.rem(spot + r, spots)), device_id_type=MESH)
    for r in range(1, outer):
        pl.semaphore_signal(barrier, inc=1, device_id=at_outer(lax.rem(group + r, outer)), device_id_type=MESH)

    for copy in copies_in:
        copy.wait()

    matrix = mix_ref[...]
    left = ROTATION_ITERS

    obs = sens_ref.shape[1]
    column = jnp.broadcast_to(sens_ref[...].astype(F32), (width, obs)).T
    values = jnp.broadcast_to(value_ref[...], (width, obs)).T
    lane = lax.broadcasted_iota(jnp.int32, (obs, width), 1).astype(F32)
    tiles = rows_ref.shape[0] // width
    picked, prec = jnp.zeros((obs, 2 * width), F32), jnp.zeros((obs, width), F32)
    for k in range(0, tiles, 2):
        hot = []
        for t in (k, k + 1):
            hit = (column - float(t * width)) == lane
            hot.append(jnp.where(hit, 1.0, 0.0).astype(BF16))
            prec = prec + jnp.where(hit, prec_ref[:, t * width : (t + 1) * width], 0.0)
        picked = picked + dot(cat(hot, 1), lhs2(rows_ref[k * width : (k + 2) * width, :]))
        if k % 4 == 0 and ROTATION_ITERS - left < early - 2:
            matrix, left = polish_step(matrix), left - 1
    gain = values * jnp.sum(prec, axis=1, keepdims=True)
    contrib = (halves(picked) * gain).astype(BF16)

    block, offset = block_ref[...], offset_ref[...]
    place = ((lax.rem(block, inner) * cores + lax.div(offset, half)) * outer + lax.div(block, inner)) * half
    place = place + lax.rem(offset, half)
    size = outer * half
    line = lax.broadcasted_iota(jnp.int32, (size, obs), 0)
    for s in range(spots):
        part[s] = dot(jnp.where(line == place - s * size, 1.0, 0.0).astype(BF16), contrib).astype(BF16)
        if s % (spots // 2) == 0 and ROTATION_ITERS - left < early:
            matrix, left = polish_step(matrix), left - 1

    pl.semaphore_wait(barrier, spots - 1 + outer - 1)

    sent1 = []
    for r in range(1, spots):
        to = lax.rem(spot + r, spots)
        copy = pltpu.make_async_remote_copy(
            part.at[to], got1.at[spot], s_i1.at[r], r_i1.at[r], device_id=at_spot(to), device_id_type=MESH
        )
        copy.start()
        sent1.append(copy)
    got1[spot] = part[spot]

    for _ in range(left):
        matrix = polish_step(matrix)
    rotation = matrix
    turned = rotation.T
    ahead, back = rhs2(turned), rhs2(rotation)

    def decay_row(t):
        return decay_ref[t : t + 1, :]

    def advance(maps, j):
        return [halves(dot(lhs2(m), ahead)) * decay_row(c * CHUNK + j) for c, m in enumerate(maps)]

    maps = [turned * decay_row(c * CHUNK) for c in range(chunks)]
    for j in range(1, 3):
        maps = advance(maps, j)

    for copy in sent1:
        copy.wait()
    total = got1[0].astype(F32)
    for s in range(1, spots):
        total = total + got1[s].astype(F32)
    red1[...] = total.reshape(outer, half, width)
    sent2 = []
    for r in range(1, outer):
        to = lax.rem(group + r, outer)
        copy = pltpu.make_async_remote_copy(
            red1.at[to], got2.at[group], s_i2.at[r], r_i2.at[r], device_id=at_outer(to), device_id_type=MESH
        )
        copy.start()
        sent2.append(copy)
    got2[group] = red1[group]

    for j in range(3, CHUNK):
        maps = advance(maps, j)
    for copy in sent2:
        copy.wait()
    total = got2[0]
    for k in range(1, outer):
        total = total + got2[k]
    info[core] = total
    other = cores - 1 - core
    copy3 = pltpu.make_async_remote_copy(
        info.at[core], info.at[core], s_i3, r_i3, device_id={"tm": tm, "sensor": other}, device_id_type=MESH
    )
    copy3.start()

    levels = [maps]
    while len(levels[-1]) > 1:
        last = levels[-1]
        levels.append([mm(last[k], last[k + 1]) for k in range(0, len(last), 2)])

    def exchange(source, slots, me, count, send, recv, place_of):
        copies = []
        for r in range(1, count):
            copy = pltpu.make_async_remote_copy(
                source, slots.at[me], send.at[r], recv.at[r],
                device_id=place_of(lax.rem(me + r, count)), device_id_type=MESH,
            )
            copy.start()
            copies.append(copy)
        return copies

    maps1[mine] = levels[-1][0].astype(maps1.dtype)
    sent_m1 = exchange(maps1.at[mine], maps1, mine, inner, s_m1, r_m1, at_inner)

    copy3.wait()

    def strided(ref, j):
        return ref[pl.ds(j, chunks, stride=CHUNK), :]

    for c in range(cores):
        smooth[c * half : (c + 1) * half, :] = info[c]
    news = [strided(smooth, j) for j in range(CHUNK)]
    fades = [strided(decay_ref, j) for j in range(CHUNK)]

    def forward_scan(enter):
        out, state = [], enter
        for j in range(CHUNK):
            if state is None:
                state = news[j]
            else:
                state = halves(dot(lhs2(state), ahead)) * fades[j] + news[j]
            out.append(state)
        return out

    def backward_scan(arrive):
        out, message = [None] * CHUNK, arrive
        for j in reversed(range(CHUNK)):
            value = news[j] if message is None else news[j] + message
            out[j] = value
            if j > 0 or arrive is None:
                message = halves(dot(lhs2(value * fades[j]), back))
        return out, message

    first = forward_scan(None)[-1]
    second = backward_scan(None)[1]
    fronts = [[first[c : c + 1] for c in range(chunks)]]
    tails = [[second[c : c + 1] for c in range(chunks)]]
    for depth in range(len(levels) - 1):
        f, b, m = fronts[-1], tails[-1], levels[depth]
        fronts.append([mm(f[k], m[k + 1]) + f[k + 1] for k in range(0, len(m), 2)])
        tails.append([mm_nt(b[k + 1], m[k]) + b[k] for k in range(0, len(m), 2)])

    def eight(f, b):
        return cat([f, b, jnp.zeros((6, width), F32)], 0)

    vecs1[mine] = eight(fronts[-1][0], tails[-1][0])
    sent_v1 = exchange(vecs1.at[mine], vecs1, mine, inner, s_v1, r_v1, at_inner)
    for copy in sent_m1:
        copy.wait()

    tree = [[maps1[k].astype(F32) for k in range(inner)]]
    bases, base = [], 0
    while len(tree[-1]) > (1 if outer > 2 else 2):
        last = tree[-1]
        tree.append([mm(last[k], last[k + 1]) for k in range(0, len(last), 2)])
        bases.append(base)
        for k, m in enumerate(tree[-1]):
            pairs[base + k] = m
        base += len(tree[-1])
    sent_m2 = []
    if outer > 2:
        maps2[group] = tree[-1][0]
        sent_m2 = exchange(maps2.at[group], maps2, group, outer, s_m2, r_m2, at_outer)
    for copy in sent_v1:
        copy.wait()
    f = [vecs1[k][0:1] for k in range(inner)]
    b = [vecs1[k][1:2] for k in range(inner)]
    depths, base = inner.bit_length() - 1, 0
    rows2_bases = []
    for depth in range(depths):
        m = tree[depth]
        f, b = (
            [mm(f[k], m[k + 1]) + f[k + 1] for k in range(0, len(m), 2)],
            [mm_nt(b[k + 1], m[k]) + b[k] for k in range(0, len(m), 2)],
        )
        rows2_bases.append(base)
        for k in range(len(f)):
            rows2[base + k] = eight(f[k], b[k])
        base += len(f)
    vecs2[group] = eight(f[0], b[0])
    sent_v2 = exchange(vecs2.at[group], vecs2, group, outer, s_v2, r_v2, at_outer)

    eye = (
        lax.broadcasted_iota(jnp.int32, (width + 8, width), 0) == lax.broadcasted_iota(jnp.int32, (width + 8, width), 1)
    ).astype(F32)
    to_here, from_here = eye, eye
    for depth in reversed(range(depths)):
        node = lax.div(mine, 1 << depth)
        bit = lax.rem(node, 2)
        even = node - bit
        if depth == 0:
            m0, m1, v0, v1 = maps1[even].astype(F32), maps1[even + 1].astype(F32), vecs1[even], vecs1[even + 1]
        else:
            m0, m1 = pairs[bases[depth - 1] + even], pairs[bases[depth - 1] + even + 1]
            v0, v1 = rows2[rows2_bases[depth - 1] + even], rows2[rows2_bases[depth - 1] + even + 1]
        pad = jnp.zeros((width, width), F32)
        to_here = jnp.where(bit == 1, mm(to_here, m0) + cat([pad, v0], 0), to_here)
        from_here = jnp.where(bit == 0, mm_nt(from_here, m1) + cat([pad, v1], 0), from_here)

    for copy in sent_m2 + sent_v2:
        copy.wait()

    zero = jnp.zeros((1, width), F32)
    enter = jnp.where(group > 0, vecs2[0][0:1], zero)
    arrive = jnp.where(group < outer - 1, vecs2[outer - 1][1:2], zero)
    for k in range(1, outer - 1):
        enter = jnp.where(k < group, mm(enter, maps2[k]) + vecs2[k][0:1], enter)
        j = outer - 1 - k
        arrive = jnp.where(j > group, mm_nt(arrive, maps2[j]) + vecs2[j][1:2], arrive)
    enter = mm(enter, to_here[:width]) + to_here[width : width + 1]
    arrive = mm(arrive, from_here[:width]) + from_here[width + 1 : width + 2]

    starts, ends = [enter], [arrive]
    for depth in reversed(range(len(levels) - 1)):
        m, f, b = levels[depth], fronts[depth], tails[depth]
        starts = [x for k, e in enumerate(starts) for x in (e, mm(e, m[2 * k]) + f[2 * k])]
        ends = [x for k, e in enumerate(ends) for x in (mm_nt(e, m[2 * k + 1]) + b[2 * k + 1], e)]
    start, end = cat(starts, 0), cat(ends, 0)
    forward = forward_scan_from(start, ahead, fades, news)
    backward = backward_scan(end)[0]
    for j in range(CHUNK):
        smooth[pl.ds(j, chunks, stride=CHUNK), :] = forward[j] + backward[j] - news[j]
    out_ref[...] = mm(smooth[...], combine_ref[...])


def forward_scan_from(state, ahead, fades, news):
    out = []
    for fade, new in zip(fades, news):
        state = halves(dot(lhs2(state), ahead)) * fade + new
        out.append(state)
    return out


def local(sensor_rows, sensor_prec, obs_sensor, obs_value, obs_block, obs_offset, decay, mix_raw, combine):
    peers, cores = lax.axis_size("tm"), lax.axis_size("sensor")
    inner = min(8, peers // 2)
    outer = peers // inner
    steps, width = decay.shape
    half = steps // cores
    spots = inner * cores
    dma = pltpu.SemaphoreType.DMA
    obs = obs_sensor.shape[0]
    arrays = (
        sensor_rows, sensor_prec.reshape(1, -1), obs_sensor.reshape(1, obs), obs_value.reshape(1, obs),
        obs_block.reshape(1, obs), obs_offset.reshape(1, obs), decay, mix_raw, combine,
    )
    return pl.pallas_call(
        functools.partial(kernel, inner, outer, cores, 6),
        out_shape=jax.ShapeDtypeStruct((steps, width), F32),
        in_specs=[pl.BlockSpec(memory_space=pltpu.HBM)] * 9,
        out_specs=pl.BlockSpec(memory_space=pltpu.VMEM),
        scratch_shapes=[pltpu.VMEM(x.shape, x.dtype) for x in arrays] + [
            dma((9,)),
            pltpu.VMEM((spots, outer * half, width), BF16),
            pltpu.VMEM((spots, outer * half, width), BF16),
            pltpu.VMEM((outer, half, width), F32),
            pltpu.VMEM((outer, half, width), F32),
            pltpu.VMEM((cores, half, width), F32),
            pltpu.VMEM((inner, width, width), BF16),
            pltpu.VMEM((inner, 8, width), F32),
            pltpu.VMEM((outer, width, width), F32),
            pltpu.VMEM((outer, 8, width), F32),
            pltpu.VMEM((steps, width), F32),
            pltpu.VMEM((inner, width, width), F32),
            pltpu.VMEM((inner, 8, width), F32),
            dma((spots,)), dma((spots,)), dma((outer,)), dma((outer,)), dma, dma,
            dma((inner,)), dma((inner,)), dma((inner,)), dma((inner,)),
            dma((outer,)), dma((outer,)), dma((outer,)), dma((outer,)),
        ],
        compiler_params=pltpu.CompilerParams(
            collective_id=0, has_side_effects=True, vmem_limit_bytes=60 * 1024 * 1024
        ),
    )(*arrays)


def solution(mesh):
    placed = (
        P("sensor", None), P("sensor"), P(("tm", "sensor")), P(("tm", "sensor")),
        P(("tm", "sensor"), None), P(("tm", "sensor")), P("tm", None), P(), P(),
    )
    return jax.shard_map(local, mesh=mesh, in_specs=placed, out_specs=P("tm", None), check_vma=False)
```

```python
import functools
import math

import jax
import jax.numpy as jnp
from jax import lax
from jax.experimental import pallas as pl
from jax.experimental.pallas import tpu as pltpu
from jax.sharding import PartitionSpec as P

ROTATION_ITERS = 12
CHUNK = 8
F32, BF16 = jnp.float32, jnp.bfloat16
MESH = pl.DeviceIdType.MESH
NT = (((1,), (1,)), ((), ()))


def dot(x, y):
    return jnp.dot(x, y, preferred_element_type=F32)


def dot_nt(x, y):
    return lax.dot_general(x, y, NT, preferred_element_type=F32)


def cat(parts, axis):
    return jnp.concatenate(parts, axis=axis)


def split(x, n):
    parts = []
    for k in range(n):
        part = x.astype(BF16)
        parts.append(part)
        if k + 1 < n:
            x = x - part.astype(F32)
    return parts


def halves(z):
    w = z.shape[1] // 2
    return z[:, :w] + z[:, w:]


def lhs2(x):
    return cat(split(x, 2), 1)


def rhs2(y):
    row = cat(split(y, 2), 1)
    return cat([row, row], 0)


def rhs2_nt(y):
    a, b = split(y, 2)
    return cat([cat([a, a], 1), cat([b, b], 1)], 0)


def mm(x, y):
    return halves(dot(lhs2(x), rhs2(y)))


def mm_nt(x, y):
    return halves(dot_nt(lhs2(x), rhs2_nt(y)))


def polish_step(matrix):
    a, b, c = split(matrix, 3)
    ab, ac = cat([a, b], 1), cat([a, c], 1)
    top = dot_nt(ab, cat([cat([a, a], 1), cat([b, b], 1)], 0))
    square = (dot_nt(ac, cat([c, a], 1)) + top[:, 128:]) + top[:, :128]
    p, q, r = split(square, 3)
    top = dot(cat([p, q], 1), cat([ab, ab], 0))
    cube = (dot(cat([p, r], 1), cat([c, a], 0)) + top[:, 128:]) + top[:, :128]
    return 1.5 * matrix - 0.5 * cube


def kernel(
    inner, outer, cores, early,
    rows_hbm, prec_hbm, sens_hbm, value_hbm, block_hbm, offset_hbm, decay_hbm, mix_hbm, combine_hbm,
    out_ref,
    rows_ref, prec_ref, sens_ref, value_ref, block_ref, offset_ref, decay_ref, mix_ref, combine_ref, loads,
    part, got1, red1, got2, info, maps1, vecs1, maps2, vecs2, smooth, pairs, rows2, edge,
    s_i1, r_i1, s_i2, r_i2, s_i3, r_i3, s_m1, r_m1, s_v1, r_v1, s_m2, r_m2, s_v2, r_v2,
):
    sources = (mix_hbm, sens_hbm, value_hbm, prec_hbm, block_hbm, offset_hbm, rows_hbm, decay_hbm, combine_hbm)
    targets = (mix_ref, sens_ref, value_ref, prec_ref, block_ref, offset_ref, rows_ref, decay_ref, combine_ref)
    copies_in = []
    for k, (source, target) in enumerate(zip(sources, targets)):
        copy = pltpu.make_async_copy(source, target, loads.at[k])
        copy.start()
        copies_in.append(copy)

    steps, width = decay_ref.shape
    half = steps // cores
    chunks = steps // CHUNK
    tm, core = lax.axis_index("tm"), lax.axis_index("sensor")
    mine, group = lax.rem(tm, inner), lax.div(tm, inner)
    spot = mine * cores + core
    spots = inner * cores

    def at_spot(s):
        return {"tm": group * inner + lax.div(s, cores), "sensor": lax.rem(s, cores)}

    def at_inner(k):
        return {"tm": group * inner + k, "sensor": core}

    def at_outer(k):
        return {"tm": k * inner + mine, "sensor": core}

    def at_cross(k):
        return {"tm": (outer - 1 - group) * inner + k, "sensor": core}

    barrier = pltpu.get_barrier_semaphore()
    for r in range(1, spots):
        pl.semaphore_signal(barrier, inc=1, device_id=at_spot(lax.rem(spot + r, spots)), device_id_type=MESH)
    for r in range(1, outer):
        pl.semaphore_signal(barrier, inc=1, device_id=at_outer(lax.rem(group + r, outer)), device_id_type=MESH)

    greeted = spots - 1 + outer - 1
    if outer == 2:
        for r in range(1, inner):
            pl.semaphore_signal(barrier, inc=1, device_id=at_cross(lax.rem(mine + r, inner)), device_id_type=MESH)
        greeted += inner - 1

    for copy in copies_in:
        copy.wait()

    matrix = mix_ref[...]
    left = ROTATION_ITERS

    obs = sens_ref.shape[1]
    column = jnp.broadcast_to(sens_ref[...].astype(F32), (width, obs)).T
    values = jnp.broadcast_to(value_ref[...], (width, obs)).T
    lane = lax.broadcasted_iota(jnp.int32, (obs, width), 1).astype(F32)
    tiles = rows_ref.shape[0] // width
    picked, prec = jnp.zeros((obs, 2 * width), F32), jnp.zeros((obs, width), F32)
    for k in range(0, tiles, 2):
        hot = []
        for t in (k, k + 1):
            hit = (column - float(t * width)) == lane
            hot.append(jnp.where(hit, 1.0, 0.0).astype(BF16))
            prec = prec + jnp.where(hit, prec_ref[:, t * width : (t + 1) * width], 0.0)
        picked = picked + dot(cat(hot, 1), lhs2(rows_ref[k * width : (k + 2) * width, :]))
        if k % 4 == 0 and ROTATION_ITERS - left < early - 4:
            matrix, left = polish_step(matrix), left - 1
    gain = values * jnp.sum(prec, axis=1, keepdims=True)
    contrib = (halves(picked) * gain).astype(BF16)

    block, offset = block_ref[...], offset_ref[...]
    place = ((lax.rem(block, inner) * cores + lax.div(offset, half)) * outer + lax.div(block, inner)) * half
    place = place + lax.rem(offset, half)
    size = outer * half
    line = lax.broadcasted_iota(jnp.int32, (size, obs), 0)
    for s in range(spots):
        part[s] = dot(jnp.where(line == place - s * size, 1.0, 0.0).astype(BF16), contrib).astype(BF16)
        if s % (spots // 4) == 0 and ROTATION_ITERS - left < early:
            matrix, left = polish_step(matrix), left - 1

    pl.semaphore_wait(barrier, greeted)

    sent1 = []
    for r in range(1, spots):
        to = lax.rem(spot + r, spots)
        copy = pltpu.make_async_remote_copy(
            part.at[to], got1.at[spot], s_i1.at[r], r_i1.at[r], device_id=at_spot(to), device_id_type=MESH
        )
        copy.start()
        sent1.append(copy)
    got1[spot] = part[spot]

    for _ in range(left):
        matrix = polish_step(matrix)
    rotation = matrix
    turned = rotation.T
    ahead, back = rhs2(turned), rhs2(rotation)

    def decay_row(t):
        return decay_ref[t : t + 1, :]

    def advance(maps, j):
        return [halves(dot(lhs2(m), ahead)) * decay_row(c * CHUNK + j) for c, m in enumerate(maps)]

    maps = [turned * decay_row(c * CHUNK) for c in range(chunks)]
    for j in range(1, 3):
        maps = advance(maps, j)

    for copy in sent1:
        copy.wait()
    total = got1[0].astype(F32)
    for s in range(1, spots):
        total = total + got1[s].astype(F32)
    red1[...] = total.reshape(outer, half, width)
    sent2 = []
    for r in range(1, outer):
        to = lax.rem(group + r, outer)
        copy = pltpu.make_async_remote_copy(
            red1.at[to], got2.at[group], s_i2.at[r], r_i2.at[r], device_id=at_outer(to), device_id_type=MESH
        )
        copy.start()
        sent2.append(copy)
    got2[group] = red1[group]

    for j in range(3, CHUNK):
        maps = advance(maps, j)
    for copy in sent2:
        copy.wait()
    total = got2[0]
    for k in range(1, outer):
        total = total + got2[k]
    info[core] = total
    other = cores - 1 - core
    copy3 = pltpu.make_async_remote_copy(
        info.at[core], info.at[core], s_i3, r_i3, device_id={"tm": tm, "sensor": other}, device_id_type=MESH
    )
    copy3.start()

    levels = [maps]
    while len(levels[-1]) > 1:
        last = levels[-1]
        levels.append([mm(last[k], last[k + 1]) for k in range(0, len(last), 2)])

    def exchange(source, slots, me, count, send, recv, place_of):
        copies = []
        for r in range(1, count):
            copy = pltpu.make_async_remote_copy(
                source, slots.at[me], send.at[r], recv.at[r],
                device_id=place_of(lax.rem(me + r, count)), device_id_type=MESH,
            )
            copy.start()
            copies.append(copy)
        return copies

    maps1[mine] = levels[-1][0].astype(maps1.dtype)
    sent_m1 = exchange(maps1.at[mine], maps1, mine, inner, s_m1, r_m1, at_inner)

    copy3.wait()

    def strided(ref, j):
        return ref[pl.ds(j, chunks, stride=CHUNK), :]

    for c in range(cores):
        smooth[c * half : (c + 1) * half, :] = info[c]
    news = [strided(smooth, j) for j in range(CHUNK)]
    fades = [strided(decay_ref, j) for j in range(CHUNK)]

    def forward_scan(enter):
        out, state = [], enter
        for j in range(CHUNK):
            if state is None:
                state = news[j]
            else:
                state = halves(dot(lhs2(state), ahead)) * fades[j] + news[j]
            out.append(state)
        return out

    def backward_scan(arrive):
        out, message = [None] * CHUNK, arrive
        for j in reversed(range(CHUNK)):
            value = news[j] if message is None else news[j] + message
            out[j] = value
            if j > 0 or arrive is None:
                message = halves(dot(lhs2(value * fades[j]), back))
        return out, message

    first = forward_scan(None)[-1]
    second = backward_scan(None)[1]
    fronts = [[first[c : c + 1] for c in range(chunks)]]
    tails = [[second[c : c + 1] for c in range(chunks)]]
    for depth in range(len(levels) - 1):
        f, b, m = fronts[-1], tails[-1], levels[depth]
        fronts.append([mm(f[k], m[k + 1]) + f[k + 1] for k in range(0, len(m), 2)])
        tails.append([mm_nt(b[k + 1], m[k]) + b[k] for k in range(0, len(m), 2)])

    def eight(f, b):
        return cat([f, b, jnp.zeros((6, width), F32)], 0)

    depths = inner.bit_length() - 1

    def group_maps():
        tree = [[maps1[k].astype(F32) for k in range(inner)]]
        bases, base = [], 0
        while len(tree[-1]) > (1 if outer > 2 else 2):
            last = tree[-1]
            tree.append([mm(last[k], last[k + 1]) for k in range(0, len(last), 2)])
            bases.append(base)
            for k, m in enumerate(tree[-1]):
                pairs[base + k] = m
            base += len(tree[-1])
        return tree, bases

    def group_vectors(tree, top):
        f = [vecs1[k][0:1] for k in range(inner)]
        b = [vecs1[k][1:2] for k in range(inner)]
        base, bases = 0, []
        for depth in range(top):
            m = tree[depth]
            f, b = (
                [mm(f[k], m[k + 1]) + f[k + 1] for k in range(0, len(m), 2)],
                [mm_nt(b[k + 1], m[k]) + b[k] for k in range(0, len(m), 2)],
            )
            bases.append(base)
            for k in range(len(f)):
                rows2[base + k] = eight(f[k], b[k])
            base += len(f)
        return f, b, bases

    def walk(bases):
        for depth in reversed(range(depths)):
            node = lax.div(mine, 1 << depth)
            bit = lax.rem(node, 2)
            even = node - bit
            if depth == 0:
                yield depth, bit, even, maps1[even].astype(F32), maps1[even + 1].astype(F32)
            else:
                at = bases[depth - 1] + even
                yield depth, bit, even, pairs[at], pairs[at + 1]

    def walk_maps(bases):
        eye = (
            lax.broadcasted_iota(jnp.int32, (width, width), 0) == lax.broadcasted_iota(jnp.int32, (width, width), 1)
        ).astype(F32)
        to_here, from_here = eye, eye
        for _, bit, _, m0, m1 in walk(bases):
            to_here = jnp.where(bit == 1, mm(to_here, m0), to_here)
            from_here = jnp.where(bit == 0, mm_nt(from_here, m1), from_here)
        return to_here, from_here

    def walk_vectors(bases, rows_bases):
        near_f, near_b = jnp.zeros((1, width), F32), jnp.zeros((1, width), F32)
        for depth, bit, even, m0, m1 in walk(bases):
            if depth == 0:
                v0, v1 = vecs1[even], vecs1[even + 1]
            else:
                at = rows_bases[depth - 1] + even
                v0, v1 = rows2[at], rows2[at + 1]
            near_f = jnp.where(bit == 1, mm(near_f, m0) + v0[0:1], near_f)
            near_b = jnp.where(bit == 0, mm_nt(near_b, m1) + v1[1:2], near_b)
        return near_f, near_b

    zero = jnp.zeros((1, width), F32)
    own_f, own_b = fronts[-1][0], tails[-1][0]
    vecs1[mine] = eight(own_f, own_b)
    sent_v1 = exchange(vecs1.at[mine], vecs1, mine, inner, s_v1, r_v1, at_inner)
    for copy in sent_m1:
        copy.wait()
    tree, bases = group_maps()
    if outer == 2:
        to_here, from_here = walk_maps(bases)
        edge[...] = eight(mm_nt(own_f, from_here), mm_nt(own_b, to_here))
        sent_v2 = []
        for r in range(inner):
            copy = pltpu.make_async_remote_copy(
                edge, vecs2.at[mine], s_v2.at[r], r_v2.at[r],
                device_id=at_cross(lax.rem(mine + r, inner)), device_id_type=MESH,
            )
            copy.start()
            sent_v2.append(copy)
        for copy in sent_v1:
            copy.wait()
        _, _, rows_bases = group_vectors(tree, depths - 1)
        near_f, near_b = walk_vectors(bases, rows_bases)
        for copy in sent_v2:
            copy.wait()
        outside = vecs2[0]
        for k in range(1, inner):
            outside = outside + vecs2[k]
        enter = jnp.where(group > 0, outside[0:1], zero)
        arrive = jnp.where(group < 1, outside[1:2], zero)
    else:
        maps2[group] = tree[-1][0]
        sent_m2 = exchange(maps2.at[group], maps2, group, outer, s_m2, r_m2, at_outer)
        for copy in sent_v1:
            copy.wait()
        f, b, rows_bases = group_vectors(tree, depths)
        vecs2[group] = eight(f[0], b[0])
        sent_v2 = exchange(vecs2.at[group], vecs2, group, outer, s_v2, r_v2, at_outer)
        to_here, from_here = walk_maps(bases)
        near_f, near_b = walk_vectors(bases, rows_bases)
        for copy in sent_m2 + sent_v2:
            copy.wait()
        enter = jnp.where(group > 0, vecs2[0][0:1], zero)
        arrive = jnp.where(group < outer - 1, vecs2[outer - 1][1:2], zero)
        for k in range(1, outer - 1):
            enter = jnp.where(k < group, mm(enter, maps2[k]) + vecs2[k][0:1], enter)
            j = outer - 1 - k
            arrive = jnp.where(j > group, mm_nt(arrive, maps2[j]) + vecs2[j][1:2], arrive)
    enter = mm(enter, to_here) + near_f
    arrive = mm(arrive, from_here) + near_b

    starts, ends = [enter], [arrive]
    for depth in reversed(range(len(levels) - 1)):
        m, f, b = levels[depth], fronts[depth], tails[depth]
        starts = [x for k, e in enumerate(starts) for x in (e, mm(e, m[2 * k]) + f[2 * k])]
        ends = [x for k, e in enumerate(ends) for x in (mm_nt(e, m[2 * k + 1]) + b[2 * k + 1], e)]
    start, end = cat(starts, 0), cat(ends, 0)
    forward = forward_scan_from(start, ahead, fades, news)
    backward = backward_scan(end)[0]
    for j in range(CHUNK):
        smooth[pl.ds(j, chunks, stride=CHUNK), :] = forward[j] + backward[j] - news[j]
    out_ref[...] = mm(smooth[...], combine_ref[...])


def forward_scan_from(state, ahead, fades, news):
    out = []
    for fade, new in zip(fades, news):
        state = halves(dot(lhs2(state), ahead)) * fade + new
        out.append(state)
    return out


def local(sensor_rows, sensor_prec, obs_sensor, obs_value, obs_block, obs_offset, decay, mix_raw, combine):
    peers, cores = lax.axis_size("tm"), lax.axis_size("sensor")
    inner = min(8, peers // 2)
    outer = peers // inner
    steps, width = decay.shape
    half = steps // cores
    spots, slots = inner * cores, max(inner, outer)
    dma = pltpu.SemaphoreType.DMA
    obs = obs_sensor.shape[0]
    arrays = (
        sensor_rows, sensor_prec.reshape(1, -1), obs_sensor.reshape(1, obs), obs_value.reshape(1, obs),
        obs_block.reshape(1, obs), obs_offset.reshape(1, obs), decay, mix_raw, combine,
    )
    return pl.pallas_call(
        functools.partial(kernel, inner, outer, cores, 8),
        out_shape=jax.ShapeDtypeStruct((steps, width), F32),
        in_specs=[pl.BlockSpec(memory_space=pltpu.HBM)] * 9,
        out_specs=pl.BlockSpec(memory_space=pltpu.VMEM),
        scratch_shapes=[pltpu.VMEM(x.shape, x.dtype) for x in arrays] + [
            dma((9,)),
            pltpu.VMEM((spots, outer * half, width), BF16),
            pltpu.VMEM((spots, outer * half, width), BF16),
            pltpu.VMEM((outer, half, width), F32),
            pltpu.VMEM((outer, half, width), F32),
            pltpu.VMEM((cores, half, width), F32),
            pltpu.VMEM((inner, width, width), BF16),
            pltpu.VMEM((inner, 8, width), F32),
            pltpu.VMEM((outer, width, width), F32),
            pltpu.VMEM((slots, 8, width), F32),
            pltpu.VMEM((steps, width), F32),
            pltpu.VMEM((inner, width, width), F32),
            pltpu.VMEM((inner, 8, width), F32),
            pltpu.VMEM((8, width), F32),
            dma((spots,)), dma((spots,)), dma((outer,)), dma((outer,)), dma, dma,
            dma((inner,)), dma((inner,)), dma((inner,)), dma((inner,)),
            dma((outer,)), dma((outer,)), dma((slots,)), dma((slots,)),
        ],
        compiler_params=pltpu.CompilerParams(
            collective_id=0, has_side_effects=True, vmem_limit_bytes=60 * 1024 * 1024
        ),
    )(*arrays)


def solution(mesh):
    placed = (
        P("sensor", None), P("sensor"), P(("tm", "sensor")), P(("tm", "sensor")),
        P(("tm", "sensor"), None), P(("tm", "sensor")), P("tm", None), P(), P(),
    )
    return jax.shard_map(local, mesh=mesh, in_specs=placed, out_specs=P("tm", None), check_vma=False)
```

```python
import functools
import math

import jax
import jax.numpy as jnp
from jax import lax
from jax.experimental import pallas as pl
from jax.experimental.pallas import tpu as pltpu
from jax.sharding import PartitionSpec as P

ROTATION_ITERS = 12
CHUNK = 8
F32, BF16 = jnp.float32, jnp.bfloat16
MESH = pl.DeviceIdType.MESH
NT = (((1,), (1,)), ((), ()))


def dot(x, y):
    return jnp.dot(x, y, preferred_element_type=F32)


def dot_nt(x, y):
    return lax.dot_general(x, y, NT, preferred_element_type=F32)


def cat(parts, axis):
    return jnp.concatenate(parts, axis=axis)


def split(x, n):
    parts = []
    for k in range(n):
        part = x.astype(BF16)
        parts.append(part)
        if k + 1 < n:
            x = x - part.astype(F32)
    return parts


def halves(z):
    w = z.shape[1] // 2
    return z[:, :w] + z[:, w:]


def lhs2(x):
    return cat(split(x, 2), 1)


def rhs2(y):
    row = cat(split(y, 2), 1)
    return cat([row, row], 0)


def rhs2_nt(y):
    a, b = split(y, 2)
    return cat([cat([a, a], 1), cat([b, b], 1)], 0)


def mm(x, y):
    return halves(dot(lhs2(x), rhs2(y)))


def mm_nt(x, y):
    return halves(dot_nt(lhs2(x), rhs2_nt(y)))


def polish_step(matrix):
    a, b, c = split(matrix, 3)
    ab, ac = cat([a, b], 1), cat([a, c], 1)
    top = dot_nt(ab, cat([cat([a, a], 1), cat([b, b], 1)], 0))
    square = (dot_nt(ac, cat([c, a], 1)) + top[:, 128:]) + top[:, :128]
    p, q, r = split(square, 3)
    top = dot(cat([p, q], 1), cat([ab, ab], 0))
    cube = (dot(cat([p, r], 1), cat([c, a], 0)) + top[:, 128:]) + top[:, :128]
    return 1.5 * matrix - 0.5 * cube


def kernel(
    inner, outer, cores, early,
    rows_hbm, prec_hbm, sens_hbm, value_hbm, block_hbm, offset_hbm, decay_hbm, mix_hbm, combine_hbm,
    out_ref,
    rows_ref, prec_ref, sens_ref, value_ref, block_ref, offset_ref, decay_ref, mix_ref, combine_ref, loads,
    part, got1, red1, got2, info, maps1, vecs1, maps2, vecs2, smooth, pairs, rows2, edge,
    s_i1, r_i1, s_i2, r_i2, s_i3, r_i3, s_m1, r_m1, s_v1, r_v1, s_m2, r_m2, s_v2, r_v2,
):
    sources = (mix_hbm, sens_hbm, value_hbm, prec_hbm, block_hbm, offset_hbm, rows_hbm, decay_hbm, combine_hbm)
    targets = (mix_ref, sens_ref, value_ref, prec_ref, block_ref, offset_ref, rows_ref, decay_ref, combine_ref)
    copies_in = []
    for k, (source, target) in enumerate(zip(sources, targets)):
        copy = pltpu.make_async_copy(source, target, loads.at[k])
        copy.start()
        copies_in.append(copy)

    steps, width = decay_ref.shape
    half = steps // cores
    chunks = steps // CHUNK
    tm, core = lax.axis_index("tm"), lax.axis_index("sensor")
    mine, group = lax.rem(tm, inner), lax.div(tm, inner)
    spot = mine * cores + core
    spots = inner * cores

    def at_spot(s):
        return {"tm": group * inner + lax.div(s, cores), "sensor": lax.rem(s, cores)}

    def at_inner(k):
        return {"tm": group * inner + k, "sensor": core}

    def at_outer(k):
        return {"tm": k * inner + mine, "sensor": core}

    def at_cross(k):
        return {"tm": (outer - 1 - group) * inner + k, "sensor": core}

    barrier = pltpu.get_barrier_semaphore()
    for r in range(1, spots):
        pl.semaphore_signal(barrier, inc=1, device_id=at_spot(lax.rem(spot + r, spots)), device_id_type=MESH)
    for r in range(1, outer):
        pl.semaphore_signal(barrier, inc=1, device_id=at_outer(lax.rem(group + r, outer)), device_id_type=MESH)

    greeted = spots - 1 + outer - 1
    if outer == 2:
        for r in range(1, inner):
            pl.semaphore_signal(barrier, inc=1, device_id=at_cross(lax.rem(mine + r, inner)), device_id_type=MESH)
        greeted += inner - 1

    for copy in copies_in:
        copy.wait()

    matrix = mix_ref[...]
    left = ROTATION_ITERS

    obs = sens_ref.shape[1]
    column = jnp.broadcast_to(sens_ref[...].astype(F32), (width, obs)).T
    values = jnp.broadcast_to(value_ref[...], (width, obs)).T
    lane = lax.broadcasted_iota(jnp.int32, (obs, width), 1).astype(F32)
    tiles = rows_ref.shape[0] // width
    picked, prec = jnp.zeros((obs, 2 * width), F32), jnp.zeros((obs, width), F32)
    for k in range(0, tiles, 2):
        hot = []
        for t in (k, k + 1):
            hit = (column - float(t * width)) == lane
            hot.append(jnp.where(hit, 1.0, 0.0).astype(BF16))
            prec = prec + jnp.where(hit, prec_ref[:, t * width : (t + 1) * width], 0.0)
        picked = picked + dot(cat(hot, 1), lhs2(rows_ref[k * width : (k + 2) * width, :]))
        if ROTATION_ITERS - left < early - 4:
            matrix, left = polish_step(matrix), left - 1
    gain = values * jnp.sum(prec, axis=1, keepdims=True)
    contrib = (halves(picked) * gain).astype(BF16)

    block, offset = block_ref[...], offset_ref[...]
    place = ((lax.rem(block, inner) * cores + lax.div(offset, half)) * outer + lax.div(block, inner)) * half
    place = place + lax.rem(offset, half)
    size = outer * half
    line = lax.broadcasted_iota(jnp.int32, (size, obs), 0)
    for s in range(spots):
        part[s] = dot(jnp.where(line == place - s * size, 1.0, 0.0).astype(BF16), contrib).astype(BF16)
        if s % (spots // 4) == 0 and ROTATION_ITERS - left < early:
            matrix, left = polish_step(matrix), left - 1

    pl.semaphore_wait(barrier, greeted)

    sent1 = []
    for r in range(1, spots):
        to = lax.rem(spot + r, spots)
        copy = pltpu.make_async_remote_copy(
            part.at[to], got1.at[spot], s_i1.at[r], r_i1.at[r], device_id=at_spot(to), device_id_type=MESH
        )
        copy.start()
        sent1.append(copy)
    got1[spot] = part[spot]

    for _ in range(left):
        matrix = polish_step(matrix)
    rotation = matrix
    turned = rotation.T
    ahead, back = rhs2(turned), rhs2(rotation)

    def decay_row(t):
        return decay_ref[t : t + 1, :]

    def advance(maps, j):
        return [halves(dot(lhs2(m), ahead)) * decay_row(c * CHUNK + j) for c, m in enumerate(maps)]

    maps = [turned * decay_row(c * CHUNK) for c in range(chunks)]
    for j in range(1, CHUNK):
        maps = advance(maps, j)
    levels = [maps]
    while len(levels[-1]) > 1:
        last = levels[-1]
        levels.append([mm(last[k], last[k + 1]) for k in range(0, len(last), 2)])

    def exchange(source, slots, me, count, send, recv, place_of):
        copies = []
        for r in range(1, count):
            copy = pltpu.make_async_remote_copy(
                source, slots.at[me], send.at[r], recv.at[r],
                device_id=place_of(lax.rem(me + r, count)), device_id_type=MESH,
            )
            copy.start()
            copies.append(copy)
        return copies

    maps1[mine] = levels[-1][0].astype(maps1.dtype)
    sent_m1 = exchange(maps1.at[mine], maps1, mine, inner, s_m1, r_m1, at_inner)

    for copy in sent1:
        copy.wait()
    total = got1[0].astype(F32)
    for s in range(1, spots):
        total = total + got1[s].astype(F32)
    red1[...] = total.reshape(outer, half, width)
    sent2 = []
    for r in range(1, outer):
        to = lax.rem(group + r, outer)
        copy = pltpu.make_async_remote_copy(
            red1.at[to], got2.at[group], s_i2.at[r], r_i2.at[r], device_id=at_outer(to), device_id_type=MESH
        )
        copy.start()
        sent2.append(copy)
    got2[group] = red1[group]

    for copy in sent2:
        copy.wait()
    total = got2[0]
    for k in range(1, outer):
        total = total + got2[k]
    info[core] = total
    other = cores - 1 - core
    copy3 = pltpu.make_async_remote_copy(
        info.at[core], info.at[core], s_i3, r_i3, device_id={"tm": tm, "sensor": other}, device_id_type=MESH
    )
    copy3.start()

    def eight(f, b):
        return cat([f, b, jnp.zeros((6, width), F32)], 0)

    depths = inner.bit_length() - 1

    def group_maps():
        tree = [[maps1[k].astype(F32) for k in range(inner)]]
        bases, base = [], 0
        while len(tree[-1]) > (1 if outer > 2 else 2):
            last = tree[-1]
            tree.append([mm(last[k], last[k + 1]) for k in range(0, len(last), 2)])
            bases.append(base)
            for k, m in enumerate(tree[-1]):
                pairs[base + k] = m
            base += len(tree[-1])
        return tree, bases

    def group_vectors(tree, top):
        f = [vecs1[k][0:1] for k in range(inner)]
        b = [vecs1[k][1:2] for k in range(inner)]
        base, bases = 0, []
        for depth in range(top):
            m = tree[depth]
            f, b = (
                [mm(f[k], m[k + 1]) + f[k + 1] for k in range(0, len(m), 2)],
                [mm_nt(b[k + 1], m[k]) + b[k] for k in range(0, len(m), 2)],
            )
            bases.append(base)
            for k in range(len(f)):
                rows2[base + k] = eight(f[k], b[k])
            base += len(f)
        return f, b, bases

    def walk(bases):
        for depth in reversed(range(depths)):
            node = lax.div(mine, 1 << depth)
            bit = lax.rem(node, 2)
            even = node - bit
            if depth == 0:
                yield depth, bit, even, maps1[even].astype(F32), maps1[even + 1].astype(F32)
            else:
                at = bases[depth - 1] + even
                yield depth, bit, even, pairs[at], pairs[at + 1]

    def walk_maps(bases):
        eye = (
            lax.broadcasted_iota(jnp.int32, (width, width), 0) == lax.broadcasted_iota(jnp.int32, (width, width), 1)
        ).astype(F32)
        to_here, from_here = eye, eye
        for _, bit, _, m0, m1 in walk(bases):
            to_here = jnp.where(bit == 1, mm(to_here, m0), to_here)
            from_here = jnp.where(bit == 0, mm_nt(from_here, m1), from_here)
        return to_here, from_here

    def walk_vectors(bases, rows_bases):
        near_f, near_b = jnp.zeros((1, width), F32), jnp.zeros((1, width), F32)
        for depth, bit, even, m0, m1 in walk(bases):
            if depth == 0:
                v0, v1 = vecs1[even], vecs1[even + 1]
            else:
                at = rows_bases[depth - 1] + even
                v0, v1 = rows2[at], rows2[at + 1]
            near_f = jnp.where(bit == 1, mm(near_f, m0) + v0[0:1], near_f)
            near_b = jnp.where(bit == 0, mm_nt(near_b, m1) + v1[1:2], near_b)
        return near_f, near_b

    for copy in sent_m1:
        copy.wait()
    tree, bases = group_maps()
    to_here, from_here = walk_maps(bases)
    copy3.wait()

    def strided(ref, j):
        return ref[pl.ds(j, chunks, stride=CHUNK), :]

    for c in range(cores):
        smooth[c * half : (c + 1) * half, :] = info[c]
    news = [strided(smooth, j) for j in range(CHUNK)]
    fades = [strided(decay_ref, j) for j in range(CHUNK)]

    def forward_scan(enter):
        out, state = [], enter
        for j in range(CHUNK):
            if state is None:
                state = news[j]
            else:
                state = halves(dot(lhs2(state), ahead)) * fades[j] + news[j]
            out.append(state)
        return out

    def backward_scan(arrive):
        out, message = [None] * CHUNK, arrive
        for j in reversed(range(CHUNK)):
            value = news[j] if message is None else news[j] + message
            out[j] = value
            if j > 0 or arrive is None:
                message = halves(dot(lhs2(value * fades[j]), back))
        return out, message

    first = forward_scan(None)[-1]
    second = backward_scan(None)[1]
    fronts = [[first[c : c + 1] for c in range(chunks)]]
    tails = [[second[c : c + 1] for c in range(chunks)]]
    for depth in range(len(levels) - 1):
        f, b, m = fronts[-1], tails[-1], levels[depth]
        fronts.append([mm(f[k], m[k + 1]) + f[k + 1] for k in range(0, len(m), 2)])
        tails.append([mm_nt(b[k + 1], m[k]) + b[k] for k in range(0, len(m), 2)])

    zero = jnp.zeros((1, width), F32)
    own_f, own_b = fronts[-1][0], tails[-1][0]
    vecs1[mine] = eight(own_f, own_b)
    sent_v1 = exchange(vecs1.at[mine], vecs1, mine, inner, s_v1, r_v1, at_inner)
    if outer == 2:
        edge[...] = eight(mm_nt(own_f, from_here), mm_nt(own_b, to_here))
        sent_v2 = []
        for r in range(inner):
            copy = pltpu.make_async_remote_copy(
                edge, vecs2.at[mine], s_v2.at[r], r_v2.at[r],
                device_id=at_cross(lax.rem(mine + r, inner)), device_id_type=MESH,
            )
            copy.start()
            sent_v2.append(copy)
        for copy in sent_v1:
            copy.wait()
        _, _, rows_bases = group_vectors(tree, depths - 1)
        near_f, near_b = walk_vectors(bases, rows_bases)
        for copy in sent_v2:
            copy.wait()
        outside = vecs2[0]
        for k in range(1, inner):
            outside = outside + vecs2[k]
        enter = jnp.where(group > 0, outside[0:1], zero)
        arrive = jnp.where(group < 1, outside[1:2], zero)
    else:
        maps2[group] = tree[-1][0]
        sent_m2 = exchange(maps2.at[group], maps2, group, outer, s_m2, r_m2, at_outer)
        for copy in sent_v1:
            copy.wait()
        f, b, rows_bases = group_vectors(tree, depths)
        vecs2[group] = eight(f[0], b[0])
        sent_v2 = exchange(vecs2.at[group], vecs2, group, outer, s_v2, r_v2, at_outer)
        near_f, near_b = walk_vectors(bases, rows_bases)
        for copy in sent_m2 + sent_v2:
            copy.wait()
        enter = jnp.where(group > 0, vecs2[0][0:1], zero)
        arrive = jnp.where(group < outer - 1, vecs2[outer - 1][1:2], zero)
        for k in range(1, outer - 1):
            enter = jnp.where(k < group, mm(enter, maps2[k]) + vecs2[k][0:1], enter)
            j = outer - 1 - k
            arrive = jnp.where(j > group, mm_nt(arrive, maps2[j]) + vecs2[j][1:2], arrive)
    enter = mm(enter, to_here) + near_f
    arrive = mm(arrive, from_here) + near_b

    starts, ends = [enter], [arrive]
    for depth in reversed(range(len(levels) - 1)):
        m, f, b = levels[depth], fronts[depth], tails[depth]
        starts = [x for k, e in enumerate(starts) for x in (e, mm(e, m[2 * k]) + f[2 * k])]
        ends = [x for k, e in enumerate(ends) for x in (mm_nt(e, m[2 * k + 1]) + b[2 * k + 1], e)]
    start, end = cat(starts, 0), cat(ends, 0)
    forward = forward_scan_from(start, ahead, fades, news)
    backward = backward_scan(end)[0]
    for j in range(CHUNK):
        smooth[pl.ds(j, chunks, stride=CHUNK), :] = forward[j] + backward[j] - news[j]
    out_ref[...] = mm(smooth[...], combine_ref[...])


def forward_scan_from(state, ahead, fades, news):
    out = []
    for fade, new in zip(fades, news):
        state = halves(dot(lhs2(state), ahead)) * fade + new
        out.append(state)
    return out


def local(sensor_rows, sensor_prec, obs_sensor, obs_value, obs_block, obs_offset, decay, mix_raw, combine):
    peers, cores = lax.axis_size("tm"), lax.axis_size("sensor")
    inner = min(8, peers // 2)
    outer = peers // inner
    steps, width = decay.shape
    half = steps // cores
    spots, slots = inner * cores, max(inner, outer)
    dma = pltpu.SemaphoreType.DMA
    obs = obs_sensor.shape[0]
    arrays = (
        sensor_rows, sensor_prec.reshape(1, -1), obs_sensor.reshape(1, obs), obs_value.reshape(1, obs),
        obs_block.reshape(1, obs), obs_offset.reshape(1, obs), decay, mix_raw, combine,
    )
    return pl.pallas_call(
        functools.partial(kernel, inner, outer, cores, 12),
        out_shape=jax.ShapeDtypeStruct((steps, width), F32),
        in_specs=[pl.BlockSpec(memory_space=pltpu.HBM)] * 9,
        out_specs=pl.BlockSpec(memory_space=pltpu.VMEM),
        scratch_shapes=[pltpu.VMEM(x.shape, x.dtype) for x in arrays] + [
            dma((9,)),
            pltpu.VMEM((spots, outer * half, width), BF16),
            pltpu.VMEM((spots, outer * half, width), BF16),
            pltpu.VMEM((outer, half, width), F32),
            pltpu.VMEM((outer, half, width), F32),
            pltpu.VMEM((cores, half, width), F32),
            pltpu.VMEM((inner, width, width), BF16),
            pltpu.VMEM((inner, 8, width), F32),
            pltpu.VMEM((outer, width, width), F32),
            pltpu.VMEM((slots, 8, width), F32),
            pltpu.VMEM((steps, width), F32),
            pltpu.VMEM((inner, width, width), F32),
            pltpu.VMEM((inner, 8, width), F32),
            pltpu.VMEM((8, width), F32),
            dma((spots,)), dma((spots,)), dma((outer,)), dma((outer,)), dma, dma,
            dma((inner,)), dma((inner,)), dma((inner,)), dma((inner,)),
            dma((outer,)), dma((outer,)), dma((slots,)), dma((slots,)),
        ],
        compiler_params=pltpu.CompilerParams(
            collective_id=0, has_side_effects=True, vmem_limit_bytes=60 * 1024 * 1024
        ),
    )(*arrays)


def solution(mesh):
    placed = (
        P("sensor", None), P("sensor"), P(("tm", "sensor")), P(("tm", "sensor")),
        P(("tm", "sensor"), None), P(("tm", "sensor")), P("tm", None), P(), P(),
    )
    return jax.shard_map(local, mesh=mesh, in_specs=placed, out_specs=P("tm", None), check_vma=False)
```

```python
import functools
import math

import jax
import jax.numpy as jnp
from jax import lax
from jax.experimental import pallas as pl
from jax.experimental.pallas import tpu as pltpu
from jax.sharding import PartitionSpec as P

ROTATION_ITERS = 12
CHUNK = 8
F32, BF16 = jnp.float32, jnp.bfloat16
MESH = pl.DeviceIdType.MESH
NT = (((1,), (1,)), ((), ()))


def dot(x, y):
    return jnp.dot(x, y, preferred_element_type=F32)


def dot_nt(x, y):
    return lax.dot_general(x, y, NT, preferred_element_type=F32)


def cat(parts, axis):
    return jnp.concatenate(parts, axis=axis)


def split(x, n):
    parts = []
    for k in range(n):
        part = x.astype(BF16)
        parts.append(part)
        if k + 1 < n:
            x = x - part.astype(F32)
    return parts


def halves(z):
    w = z.shape[1] // 2
    return z[:, :w] + z[:, w:]


def lhs2(x):
    return cat(split(x, 2), 1)


def rhs2(y):
    row = cat(split(y, 2), 1)
    return cat([row, row], 0)


def rhs2_nt(y):
    a, b = split(y, 2)
    return cat([cat([a, a], 1), cat([b, b], 1)], 0)


def mm(x, y):
    return halves(dot(lhs2(x), rhs2(y)))


def mm_nt(x, y):
    return halves(dot_nt(lhs2(x), rhs2_nt(y)))


def polish_step(matrix):
    a, b, c = split(matrix, 3)
    ab, ac = cat([a, b], 1), cat([a, c], 1)
    top = dot_nt(ab, cat([cat([a, a], 1), cat([b, b], 1)], 0))
    square = (dot_nt(ac, cat([c, a], 1)) + top[:, 128:]) + top[:, :128]
    p, q, r = split(square, 3)
    top = dot(cat([p, q], 1), cat([ab, ab], 0))
    cube = (dot(cat([p, r], 1), cat([c, a], 0)) + top[:, 128:]) + top[:, :128]
    return 1.5 * matrix - 0.5 * cube


def kernel(
    inner, outer, cores, early,
    rows_hbm, prec_hbm, sens_hbm, value_hbm, block_hbm, offset_hbm, decay_hbm, mix_hbm, combine_hbm,
    out_ref,
    rows_ref, prec_ref, sens_ref, value_ref, block_ref, offset_ref, decay_ref, mix_ref, combine_ref, loads,
    part, got1, red1, got2, info, maps1, vecs1, maps2, vecs2, smooth, pairs, rows2,
    s_i1, r_i1, s_i2, r_i2, s_i3, r_i3, s_m1, r_m1, s_v1, r_v1, s_m2, r_m2, s_v2, r_v2,
):
    sources = (mix_hbm, sens_hbm, value_hbm, prec_hbm, block_hbm, offset_hbm, rows_hbm, decay_hbm, combine_hbm)
    targets = (mix_ref, sens_ref, value_ref, prec_ref, block_ref, offset_ref, rows_ref, decay_ref, combine_ref)
    copies_in = []
    for k, (source, target) in enumerate(zip(sources, targets)):
        copy = pltpu.make_async_copy(source, target, loads.at[k])
        copy.start()
        copies_in.append(copy)

    steps, width = decay_ref.shape
    half = steps // cores
    chunks = steps // CHUNK
    tm, core = lax.axis_index("tm"), lax.axis_index("sensor")
    mine, group = lax.rem(tm, inner), lax.div(tm, inner)
    spot = mine * cores + core
    spots = inner * cores

    def at_spot(s):
        return {"tm": group * inner + lax.div(s, cores), "sensor": lax.rem(s, cores)}

    def at_inner(k):
        return {"tm": group * inner + k, "sensor": core}

    def at_outer(k):
        return {"tm": k * inner + mine, "sensor": core}

    barrier = pltpu.get_barrier_semaphore()
    for r in range(1, spots):
        pl.semaphore_signal(barrier, inc=1, device_id=at_spot(lax.rem(spot + r, spots)), device_id_type=MESH)
    for r in range(1, outer):
        pl.semaphore_signal(barrier, inc=1, device_id=at_outer(lax.rem(group + r, outer)), device_id_type=MESH)

    greeted = spots - 1 + outer - 1
    for copy in copies_in:
        copy.wait()

    matrix = mix_ref[...]
    left = ROTATION_ITERS

    obs = sens_ref.shape[1]
    column = jnp.broadcast_to(sens_ref[...].astype(F32), (width, obs)).T
    values = jnp.broadcast_to(value_ref[...], (width, obs)).T
    lane = lax.broadcasted_iota(jnp.int32, (obs, width), 1).astype(F32)
    tiles = rows_ref.shape[0] // width
    picked, prec = jnp.zeros((obs, 2 * width), F32), jnp.zeros((obs, width), F32)
    for k in range(0, tiles, 2):
        hot = []
        for t in (k, k + 1):
            hit = (column - float(t * width)) == lane
            hot.append(jnp.where(hit, 1.0, 0.0).astype(BF16))
            prec = prec + jnp.where(hit, prec_ref[:, t * width : (t + 1) * width], 0.0)
        picked = picked + dot(cat(hot, 1), lhs2(rows_ref[k * width : (k + 2) * width, :]))
        if ROTATION_ITERS - left < early - 4:
            matrix, left = polish_step(matrix), left - 1
    gain = values * jnp.sum(prec, axis=1, keepdims=True)
    contrib = (halves(picked) * gain).astype(BF16)

    block, offset = block_ref[...], offset_ref[...]
    place = ((lax.rem(block, inner) * cores + lax.div(offset, half)) * outer + lax.div(block, inner)) * half
    place = place + lax.rem(offset, half)
    size = outer * half
    line = lax.broadcasted_iota(jnp.int32, (size, obs), 0)
    for s in range(spots):
        part[s] = dot(jnp.where(line == place - s * size, 1.0, 0.0).astype(BF16), contrib).astype(BF16)
        if s % (spots // 4) == 0 and ROTATION_ITERS - left < early:
            matrix, left = polish_step(matrix), left - 1

    pl.semaphore_wait(barrier, greeted)

    sent1 = []
    for r in range(1, spots):
        to = lax.rem(spot + r, spots)
        copy = pltpu.make_async_remote_copy(
            part.at[to], got1.at[spot], s_i1.at[r], r_i1.at[r], device_id=at_spot(to), device_id_type=MESH
        )
        copy.start()
        sent1.append(copy)
    got1[spot] = part[spot]

    for _ in range(left):
        matrix = polish_step(matrix)
    rotation = matrix
    turned = rotation.T
    ahead, back = rhs2(turned), rhs2(rotation)

    def decay_row(t):
        return decay_ref[t : t + 1, :]

    def advance(maps, j):
        return [halves(dot(lhs2(m), ahead)) * decay_row(c * CHUNK + j) for c, m in enumerate(maps)]

    maps = [turned * decay_row(c * CHUNK) for c in range(chunks)]
    for j in range(1, CHUNK):
        maps = advance(maps, j)
    levels = [maps]
    while len(levels[-1]) > 1:
        last = levels[-1]
        levels.append([mm(last[k], last[k + 1]) for k in range(0, len(last), 2)])

    def exchange(source, slots, me, count, send, recv, place_of):
        copies = []
        for r in range(1, count):
            copy = pltpu.make_async_remote_copy(
                source, slots.at[me], send.at[r], recv.at[r],
                device_id=place_of(lax.rem(me + r, count)), device_id_type=MESH,
            )
            copy.start()
            copies.append(copy)
        return copies

    maps1[mine] = levels[-1][0].astype(maps1.dtype)
    sent_m1 = exchange(maps1.at[mine], maps1, mine, inner, s_m1, r_m1, at_inner)

    for copy in sent1:
        copy.wait()
    total = got1[0].astype(F32)
    for s in range(1, spots):
        total = total + got1[s].astype(F32)
    red1[...] = total.reshape(outer, half, width)
    sent2 = []
    for r in range(1, outer):
        to = lax.rem(group + r, outer)
        copy = pltpu.make_async_remote_copy(
            red1.at[to], got2.at[group], s_i2.at[r], r_i2.at[r], device_id=at_outer(to), device_id_type=MESH
        )
        copy.start()
        sent2.append(copy)
    got2[group] = red1[group]

    for copy in sent2:
        copy.wait()
    total = got2[0]
    for k in range(1, outer):
        total = total + got2[k]
    info[core] = total
    other = cores - 1 - core
    copy3 = pltpu.make_async_remote_copy(
        info.at[core], info.at[core], s_i3, r_i3, device_id={"tm": tm, "sensor": other}, device_id_type=MESH
    )
    copy3.start()

    def eight(f, b):
        return cat([f, b, jnp.zeros((6, width), F32)], 0)

    depths = inner.bit_length() - 1

    def group_maps():
        tree = [[maps1[k].astype(F32) for k in range(inner)]]
        bases, base = [], 0
        while len(tree[-1]) > (1 if outer > 2 else 2):
            last = tree[-1]
            tree.append([mm(last[k], last[k + 1]) for k in range(0, len(last), 2)])
            bases.append(base)
            for k, m in enumerate(tree[-1]):
                pairs[base + k] = m
            base += len(tree[-1])
        return tree, bases

    def group_vectors(tree, top):
        f = [vecs1[k][0:1] for k in range(inner)]
        b = [vecs1[k][1:2] for k in range(inner)]
        base, bases = 0, []
        for depth in range(top):
            m = tree[depth]
            f, b = (
                [mm(f[k], m[k + 1]) + f[k + 1] for k in range(0, len(m), 2)],
                [mm_nt(b[k + 1], m[k]) + b[k] for k in range(0, len(m), 2)],
            )
            bases.append(base)
            for k in range(len(f)):
                rows2[base + k] = eight(f[k], b[k])
            base += len(f)
        return f, b, bases

    def walk(bases):
        for depth in reversed(range(depths)):
            node = lax.div(mine, 1 << depth)
            bit = lax.rem(node, 2)
            even = node - bit
            if depth == 0:
                yield depth, bit, even, maps1[even].astype(F32), maps1[even + 1].astype(F32)
            else:
                at = bases[depth - 1] + even
                yield depth, bit, even, pairs[at], pairs[at + 1]

    def walk_maps(bases):
        eye = (
            lax.broadcasted_iota(jnp.int32, (width, width), 0) == lax.broadcasted_iota(jnp.int32, (width, width), 1)
        ).astype(F32)
        to_here, from_here = eye, eye
        for _, bit, _, m0, m1 in walk(bases):
            to_here = jnp.where(bit == 1, mm(to_here, m0), to_here)
            from_here = jnp.where(bit == 0, mm_nt(from_here, m1), from_here)
        return to_here, from_here

    def walk_vectors(bases, rows_bases):
        near_f, near_b = jnp.zeros((1, width), F32), jnp.zeros((1, width), F32)
        for depth, bit, even, m0, m1 in walk(bases):
            if depth == 0:
                v0, v1 = vecs1[even], vecs1[even + 1]
            else:
                at = rows_bases[depth - 1] + even
                v0, v1 = rows2[at], rows2[at + 1]
            near_f = jnp.where(bit == 1, mm(near_f, m0) + v0[0:1], near_f)
            near_b = jnp.where(bit == 0, mm_nt(near_b, m1) + v1[1:2], near_b)
        return near_f, near_b

    for copy in sent_m1:
        copy.wait()
    tree, bases = group_maps()
    to_here, from_here = walk_maps(bases)
    copy3.wait()

    def strided(ref, j):
        return ref[pl.ds(j, chunks, stride=CHUNK), :]

    for c in range(cores):
        smooth[c * half : (c + 1) * half, :] = info[c]
    news = [strided(smooth, j) for j in range(CHUNK)]
    fades = [strided(decay_ref, j) for j in range(CHUNK)]

    def forward_scan(enter):
        out, state = [], enter
        for j in range(CHUNK):
            if state is None:
                state = news[j]
            else:
                state = halves(dot(lhs2(state), ahead)) * fades[j] + news[j]
            out.append(state)
        return out

    def backward_scan(arrive):
        out, message = [None] * CHUNK, arrive
        for j in reversed(range(CHUNK)):
            value = news[j] if message is None else news[j] + message
            out[j] = value
            if j > 0 or arrive is None:
                message = halves(dot(lhs2(value * fades[j]), back))
        return out, message

    first = forward_scan(None)[-1]
    second = backward_scan(None)[1]
    fronts = [[first[c : c + 1] for c in range(chunks)]]
    tails = [[second[c : c + 1] for c in range(chunks)]]
    for depth in range(len(levels) - 1):
        f, b, m = fronts[-1], tails[-1], levels[depth]
        fronts.append([mm(f[k], m[k + 1]) + f[k + 1] for k in range(0, len(m), 2)])
        tails.append([mm_nt(b[k + 1], m[k]) + b[k] for k in range(0, len(m), 2)])

    zero = jnp.zeros((1, width), F32)
    own_f, own_b = fronts[-1][0], tails[-1][0]
    vecs1[mine] = eight(own_f, own_b)
    sent_v1 = exchange(vecs1.at[mine], vecs1, mine, inner, s_v1, r_v1, at_inner)
    sent_m2 = []
    if outer > 2:
        maps2[group] = tree[-1][0]
        sent_m2 = exchange(maps2.at[group], maps2, group, outer, s_m2, r_m2, at_outer)
    for copy in sent_v1:
        copy.wait()
    f, b, rows_bases = group_vectors(tree, depths)
    vecs2[group] = eight(f[0], b[0])
    sent_v2 = exchange(vecs2.at[group], vecs2, group, outer, s_v2, r_v2, at_outer)
    near_f, near_b = walk_vectors(bases, rows_bases)
    for copy in sent_m2 + sent_v2:
        copy.wait()
    enter = jnp.where(group > 0, vecs2[0][0:1], zero)
    arrive = jnp.where(group < outer - 1, vecs2[outer - 1][1:2], zero)
    for k in range(1, outer - 1):
        enter = jnp.where(k < group, mm(enter, maps2[k]) + vecs2[k][0:1], enter)
        j = outer - 1 - k
        arrive = jnp.where(j > group, mm_nt(arrive, maps2[j]) + vecs2[j][1:2], arrive)
    enter = mm(enter, to_here) + near_f
    arrive = mm(arrive, from_here) + near_b

    starts, ends = [enter], [arrive]
    for depth in reversed(range(len(levels) - 1)):
        m, f, b = levels[depth], fronts[depth], tails[depth]
        starts = [x for k, e in enumerate(starts) for x in (e, mm(e, m[2 * k]) + f[2 * k])]
        ends = [x for k, e in enumerate(ends) for x in (mm_nt(e, m[2 * k + 1]) + b[2 * k + 1], e)]
    start, end = cat(starts, 0), cat(ends, 0)
    forward = forward_scan_from(start, ahead, fades, news)
    backward = backward_scan(end)[0]
    for j in range(CHUNK):
        smooth[pl.ds(j, chunks, stride=CHUNK), :] = forward[j] + backward[j] - news[j]
    out_ref[...] = mm(smooth[...], combine_ref[...])


def forward_scan_from(state, ahead, fades, news):
    out = []
    for fade, new in zip(fades, news):
        state = halves(dot(lhs2(state), ahead)) * fade + new
        out.append(state)
    return out


def local(sensor_rows, sensor_prec, obs_sensor, obs_value, obs_block, obs_offset, decay, mix_raw, combine):
    peers, cores = lax.axis_size("tm"), lax.axis_size("sensor")
    inner = min(8, peers // 2)
    outer = peers // inner
    steps, width = decay.shape
    half = steps // cores
    spots, slots = inner * cores, max(inner, outer)
    dma = pltpu.SemaphoreType.DMA
    obs = obs_sensor.shape[0]
    arrays = (
        sensor_rows, sensor_prec.reshape(1, -1), obs_sensor.reshape(1, obs), obs_value.reshape(1, obs),
        obs_block.reshape(1, obs), obs_offset.reshape(1, obs), decay, mix_raw, combine,
    )
    return pl.pallas_call(
        functools.partial(kernel, inner, outer, cores, 12),
        out_shape=jax.ShapeDtypeStruct((steps, width), F32),
        in_specs=[pl.BlockSpec(memory_space=pltpu.HBM)] * 9,
        out_specs=pl.BlockSpec(memory_space=pltpu.VMEM),
        scratch_shapes=[pltpu.VMEM(x.shape, x.dtype) for x in arrays] + [
            dma((9,)),
            pltpu.VMEM((spots, outer * half, width), BF16),
            pltpu.VMEM((spots, outer * half, width), BF16),
            pltpu.VMEM((outer, half, width), F32),
            pltpu.VMEM((outer, half, width), F32),
            pltpu.VMEM((cores, half, width), F32),
            pltpu.VMEM((inner, width, width), BF16),
            pltpu.VMEM((inner, 8, width), F32),
            pltpu.VMEM((outer, width, width), F32),
            pltpu.VMEM((slots, 8, width), F32),
            pltpu.VMEM((steps, width), F32),
            pltpu.VMEM((inner, width, width), F32),
            pltpu.VMEM((inner, 8, width), F32),
            dma((spots,)), dma((spots,)), dma((outer,)), dma((outer,)), dma, dma,
            dma((inner,)), dma((inner,)), dma((inner,)), dma((inner,)),
            dma((outer,)), dma((outer,)), dma((slots,)), dma((slots,)),
        ],
        compiler_params=pltpu.CompilerParams(
            collective_id=0, has_side_effects=True, vmem_limit_bytes=60 * 1024 * 1024
        ),
    )(*arrays)


def solution(mesh):
    placed = (
        P("sensor", None), P("sensor"), P(("tm", "sensor")), P(("tm", "sensor")),
        P(("tm", "sensor"), None), P(("tm", "sensor")), P("tm", None), P(), P(),
    )
    return jax.shard_map(local, mesh=mesh, in_specs=placed, out_specs=P("tm", None), check_vma=False)
```
